512 devices in a mesh: sky: 64 (over z, y_hi, core), epoch: 8 (over y_lo, x).
Axes of the slice: x: 4, y: 8 (y_hi: 4, y_lo: 2; y = y_hi * 2 + y_lo), z: 8, core: 2. Of those that a mesh axis runs over, the one named last changes fastest.
Arguments:
- visits: float32 [8, 8192, 1024], P('epoch', 'sky'), may hold values from -6 to 6
- template: float32 [8192, 1024], P(('sky', 'epoch')), may hold values from -6 to 6
- basis_taps: float32 [2, 27, 17], replicated, may hold values from -1.5 to 1.5
- coeffs: float32 [8, 64, 27, 3], P('epoch', 'sky'), may hold values from -1.2 to 1.2
- psf_taps: float32 [8, 9], P('epoch'), may hold values from -2 to 2
- inv_var: float32 [8, 8192, 1024], P('epoch', 'sky'), may hold values from 0.3 to 3
- shifts: int32 [64, 24, 8, 2], P('sky'), may hold values from -16 to 16
- vel_count: int32 [64], P('sky'), may hold values from 1 to 24, 768 in all
Outputs:
- best_map: float32 [8192, 1024], P(('sky', 'epoch'))
The draws below stay inside these ranges and needn't reach their ends.
Inputs may be any that keep to these rules, and one draw needn't show every extreme that they name: `shifts`: a velocity's shift of one epoch, row first, in whole pixels. Velocities 0 to vel_count - 1 of a tile are searched; some tile searches all 24.
All inputs are finite; a program needn't handle non-finite values. No bound on the sum of `vel_count` on one device may be relied on, other than what follows from the above.
Results may differ from the reference program's by a relative error of at most 0.0026.
Values may be sent and summed in bfloat16 or wider, within the bound.
No kernel may reach another device: no remote copies, remote signals or barrier semaphores. Data moves between devices by JAX's collectives and lax.ppermute only.
A program may use at most 64 MiB of HBM per device.

```python
import math
import jax
import jax.numpy as jnp
import numpy as np
from jax import lax

H = 128
W = 1024
NB = 27
R = 8
F = 4
SMAX = 16
NV = 24
EPOCHS = 8
TILES = 64


def set_ends(values, stream_key, least, largest):
    longest = values.shape.index(max(values.shape))
    spots = []
    for shift in (0, 1):
        where = [jax.random.randint(jax.random.fold_in(stream_key, axis), (), 0, length) for axis, length in enumerate(values.shape)]
        where[longest] = (where[longest] + shift) % values.shape[longest]
        spots.append(tuple(where))
    return values.at[spots[0]].set(least).at[spots[1]].set(largest)


def block_scale(rng, extent, pieces, smallest, top_value):
    loudness = 1.0
    for axis_at, blocks in pieces:
        heights = jax.random.uniform(jax.random.fold_in(jax.random.fold_in(rng, 6), axis_at), (blocks,), jnp.float32, smallest / len(pieces), top_value / len(pieces))
        loudness = loudness * jnp.repeat(jnp.exp(heights), extent[axis_at] // blocks).reshape((-1,) + (1,) * (len(extent) - 1 - axis_at))
    return loudness


def length_profile(count, total, bound, lean):
    weights = [(1 << 20) // math.isqrt(rank ** lean) + 1 for rank in range(2, count + 1)]
    spare, counts = total - bound - (count - 1), [1] * (count - 1)
    while spare > 0:
        movable = [i for i in range(count - 1) if counts[i] < bound]
        pool, remaining = sum([weights[i] for i in movable]), spare
        for i in movable:
            more = min(bound - counts[i], max(1, remaining * weights[i] // pool), spare)
            counts[i] = counts[i] + more
            spare = spare - more
    return np.array([bound] + counts)


def ragged(own_key, amount, total, bound, lean):
    if amount == 2:
        one = jax.random.randint(own_key, (), max(1, total - bound), min(bound, total - 1) + 1)
        return jnp.stack([one, total - one])
    sizes = jnp.asarray(length_profile(amount, total, bound, lean), jnp.int32)
    twos = (amount - 1) // 2
    source_of, sink = sizes[1:1 + 2 * twos:2], sizes[2:2 + 2 * twos:2]
    slack = jnp.minimum(source_of - 1, bound - sink)
    moved = jax.random.randint(jax.random.fold_in(own_key, 1), (twos,), 0, 1 << 20) % (slack + 1)
    sizes = sizes.at[1:1 + 2 * twos:2].set(source_of - moved).at[2:2 + 2 * twos:2].set(sink + moved)
    return sizes[jax.random.permutation(jax.random.fold_in(own_key, 2), amount)]


def bell_draw(key, extent, width, limit, pieces=(), kind=jnp.bfloat16):
    gain = block_scale(key, extent, pieces, -0.22, 0.18) if pieces else 1.0
    entries = jax.random.normal(key, extent, jnp.float32) * width * gain
    return jnp.minimum(jnp.maximum(entries, -limit), limit).astype(kind)


def setup_inputs(seed: int = 0) -> dict:
    key_of = jax.random.split(jax.random.key(seed), 9)
    visits = bell_draw(key_of[0], (EPOCHS, TILES * H, W), 1.0, 6.0, ((0, 8), (1, 64)), jnp.float32)
    template = bell_draw(key_of[1], (TILES * H, W), 1.0, 6.0, ((0, 512),), jnp.float32)
    basis_taps = bell_draw(key_of[2], (2, NB, 2 * R + 1), (2 * R + 1) ** -0.5, 1.5, (), jnp.float32)
    coeffs = bell_draw(key_of[3], (EPOCHS, TILES, NB, 3), 0.2, 1.2, ((0, 8), (1, 64)), jnp.float32)
    psf_taps = bell_draw(key_of[4], (EPOCHS, 2 * F + 1), (2 * F + 1) ** -0.5, 2.0, ((0, 8),), jnp.float32)
    inv_var = jnp.clip(jnp.exp(math.log(3.0) - 2.3025851 * jax.random.uniform(key_of[5], (EPOCHS, TILES * H, W), jnp.float32) ** block_scale(key_of[5], (EPOCHS, TILES * H, W), ((0, 8), (1, 64)), -0.2, 0.2)), 0.3, 3.0)
    shifts = set_ends(jax.random.randint(key_of[6], (TILES, NV, EPOCHS, 2), 0 - SMAX, SMAX + 1), jax.random.fold_in(key_of[6], 1), 0 - SMAX, SMAX).astype(jnp.int32)
    vel_count = ragged(key_of[7], TILES, TILES * NV // 2, NV, 2).astype(jnp.int32)
    return dict(visits=visits, template=template, basis_taps=basis_taps, coeffs=coeffs, psf_taps=psf_taps, inv_var=inv_var, shifts=shifts, vel_count=vel_count)


def conv_rows(extended, kernel, half_width):
    height = extended.shape[0] - 2 * half_width
    result = kernel[0] * extended[0:height]
    for offset in range(1, 2 * half_width + 1):
        result = result + kernel[offset] * extended[offset:offset + height]
    return result

def conv_cols(image, kernel, half_width):
    columns = image.shape[1]
    padded = jnp.pad(image, ((0, 0), (half_width, half_width)))
    result = kernel[0] * padded[:, 0:columns]
    for offset in range(1, 2 * half_width + 1):
        result = result + kernel[offset] * padded[:, offset:offset + columns]
    return result

def normalized(position, length):
    return (position - (length - 1) / 2.0) / ((length - 1) / 2.0)

def reference(visits, template, basis_taps, coeffs, psf_taps, inv_var, shifts, vel_count):
    rows = template.shape[0]
    columns = template.shape[1]
    extended = jnp.pad(template, ((R, R), (0, 0)))
    basis_maps = [conv_cols(conv_rows(extended, basis_taps[0, basis_index], R), basis_taps[1, basis_index], R) for basis_index in range(NB)]
    row_pos = normalized((jnp.arange(rows, dtype=jnp.int32) % H).astype(jnp.float32), H)[:, None]
    col_pos = normalized(jnp.arange(columns, dtype=jnp.int32).astype(jnp.float32), columns)[None, :]
    filtered_list = []
    weight_sum = jnp.zeros((TILES,), jnp.float32)
    for epoch_index in range(EPOCHS):
        per_row = jnp.repeat(coeffs[epoch_index], H, axis=0)
        model = jnp.zeros((rows, columns), jnp.float32)
        for basis_index in range(NB):
            spatial = per_row[:, basis_index, 0:1] + per_row[:, basis_index, 1:2] * col_pos + per_row[:, basis_index, 2:3] * row_pos
            model = model + spatial * basis_maps[basis_index]
        difference = visits[epoch_index] - model
        smoothed = conv_cols(conv_rows(jnp.pad(difference, ((F, F), (0, 0))), psf_taps[epoch_index], F), psf_taps[epoch_index], F)
        filtered_list.append((smoothed * inv_var[epoch_index]).astype(jnp.bfloat16))
        psf_power = jnp.sum(psf_taps[epoch_index] * psf_taps[epoch_index])
        weight_sum = weight_sum + psf_power * psf_power * lax.optimization_barrier(jnp.mean(inv_var[epoch_index].reshape(TILES, H, columns), axis=(1, 2)))
    scale_norm = jnp.sqrt(weight_sum)
    padded = jnp.pad(jnp.stack(filtered_list), ((0, 0), (SMAX, SMAX), (SMAX, SMAX)))

    def tile_search(tile_index):

        def visit_velocity(vel_index, best_map):
            total = jnp.zeros((H, columns), jnp.float32)
            for epoch_index in range(EPOCHS):
                shift_row = shifts[tile_index, vel_index, epoch_index, 0]
                shift_col = shifts[tile_index, vel_index, epoch_index, 1]
                window = lax.dynamic_slice(padded[epoch_index], (tile_index * H + SMAX + shift_row, SMAX + shift_col), (H, columns))
                total = total + window.astype(jnp.float32)
            candidate = total / scale_norm[tile_index]
            return jnp.where(vel_index < vel_count[tile_index], jnp.maximum(best_map, candidate), best_map)
        return lax.fori_loop(jnp.int32(0), jnp.int32(NV), visit_velocity, jnp.full((H, columns), -1e+30, jnp.float32))
    return lax.map(tile_search, jnp.arange(TILES, dtype=jnp.int32)).reshape(rows, columns)
```

```python
import jax
import jax.numpy as jnp
from jax import lax
from jax.experimental import pallas as pl
from jax.experimental.pallas import tpu as pltpu
from jax.sharding import PartitionSpec as P

NB = 27
R = 8
F = 4
SMAX = 16
NV = 24
EPOCHS = 8
H = 128
W = 1024
BAND = 16
TAPS = 2 * R + 1
PTAPS = 2 * F + 1
VEDGE = 24
HALF = 64 + VEDGE
WIN = 128
EXT = 192
PADW = W + 128
f32 = jnp.float32
bf16 = jnp.bfloat16


def filter_kernel(psf, visits, inv_var, above, below, bands, coeffs, col_taps, row_taps,
                  out, shifted_hi, shifted_lo, lhs_hi, lhs_lo, diff):
    tile_coeffs = (above[40:48, 0:128], coeffs[...], below[40:48, 0:128])
    vectors = []
    for c in tile_coeffs:
        vectors.append([
            jnp.dot(col_taps[...] * c[p:p + 1, :], row_taps[...],
                    precision=lax.Precision.HIGHEST, preferred_element_type=f32)
            for p in range(3)
        ])
    row = lax.broadcasted_iota(jnp.int32, (HALF, WIN), 0)
    top_row = jnp.where(row < VEDGE, row + H - VEDGE, row - VEDGE).astype(f32)
    low_row = jnp.where(row < 64, row + 64, row - 64).astype(f32)
    middle = (H - 1) / 2.0
    for block in range(2):
        w = ((top_row if block == 0 else low_row) - middle) / middle
        for l in range(TAPS):
            parts = []
            for p in range(3):
                first, second = (vectors[0][p], vectors[1][p]) if block == 0 else (vectors[1][p], vectors[2][p])
                split = VEDGE if block == 0 else 64
                parts.append(jnp.concatenate([
                    jnp.broadcast_to(first[l:l + 1, :], (split, WIN)),
                    jnp.broadcast_to(second[l:l + 1, :], (HALF - split, WIN)),
                ], axis=0))
            start = 0 if block == 0 else VEDGE
            even = pltpu.roll(parts[0] + w * parts[2], start, 1, stride=1, stride_axis=0)
            odd = pltpu.roll(parts[1], start, 1, stride=1, stride_axis=0)
            both = jnp.concatenate([even, odd], axis=0)
            hi = both.astype(bf16)
            lhs_hi[block, :, l * WIN:(l + 1) * WIN] = hi
            lhs_lo[block, :, l * WIN:(l + 1) * WIN] = (both - hi.astype(f32)).astype(bf16)

    lane = lax.broadcasted_iota(jnp.int32, (BAND, W), 1)

    def shift_band(place, band):
        for l in range(TAPS):
            s = l - R
            moved = band if s == 0 else pltpu.roll(band, (-s) % W, 1)
            if s > 0:
                moved = jnp.where(lane < W - s, moved, 0.0)
            if s < 0:
                moved = jnp.where(lane >= -s, moved, 0.0)
            hi = moved.astype(bf16)
            shifted_hi[l, place * BAND:(place + 1) * BAND, :] = hi
            shifted_lo[l, place * BAND:(place + 1) * BAND, :] = (moved - hi.astype(f32)).astype(bf16)

    for place in range(12):
        if place < 2:
            band = bands[6 + place, 16:32, :]
        elif place < 10:
            band = bands[place - 2, 0:16, :]
        else:
            band = bands[place - 10, 16:32, :]
        shift_band(place, band)

    half_width = (W - 1) / 2.0
    for block in range(2):
        for n in range(4):
            cols = slice(n * 256, (n + 1) * 256)
            rows = slice(0, WIN) if block == 0 else slice(EXT - WIN, EXT)
            rhs_hi = shifted_hi[:, rows, cols].reshape(TAPS * WIN, 256)
            rhs_lo = shifted_lo[:, rows, cols].reshape(TAPS * WIN, 256)
            acc = jnp.dot(lhs_hi[block], rhs_hi, preferred_element_type=f32)
            acc = acc + jnp.dot(lhs_lo[block], rhs_hi, preferred_element_type=f32)
            acc = acc + jnp.dot(lhs_hi[block], rhs_lo, preferred_element_type=f32)
            col = lax.broadcasted_iota(jnp.int32, (HALF, 256), 1) + n * 256
            u = (col.astype(f32) - half_width) / half_width
            model = acc[0:HALF] + u * acc[HALF:2 * HALF]
            if block == 0:
                diff[0:VEDGE, cols] = above[0:VEDGE, cols] - model[0:VEDGE]
                diff[VEDGE:HALF, cols] = visits[0:64, cols] - model[VEDGE:HALF]
            else:
                diff[HALF:HALF + 64, cols] = visits[64:128, cols] - model[0:64]
                diff[HALF + 64:2 * HALF, cols] = below[0:VEDGE, cols] - model[64:HALF]

    for c in range(10):
        smooth = psf[0] * diff[16 * c + 4:16 * c + 20, :]
        for k in range(1, PTAPS):
            smooth = smooth + psf[k] * diff[16 * c + 4 + k:16 * c + 20 + k, :]
        total = psf[F] * smooth
        for k in range(PTAPS):
            s = k - F
            if s == 0:
                continue
            moved = pltpu.roll(smooth, (-s) % W, 1)
            moved = jnp.where(lane < W - s, moved, 0.0) if s > 0 else jnp.where(lane >= -s, moved, 0.0)
            total = total + psf[k] * moved
        if c == 0:
            weight = above[24:40, :]
        elif c == 9:
            weight = below[24:40, :]
        else:
            weight = inv_var[16 * (c - 1):16 * c, :]
        rounded = (total * weight).astype(bf16)
        for part in range(3):
            owner = c - part
            if 0 <= owner < EPOCHS:
                out[owner, part * 16:(part + 1) * 16, :] = rounded


def search_kernel(count, shifts, scale, windows, out, padded, rolled):
    for e in range(EPOCHS):
        padded[e, :, W:PADW] = jnp.zeros((3 * BAND, PADW - W), f32)
        padded[e, :, 0:W] = windows[e].astype(f32)
    for r in range(8):
        for e in range(EPOCHS):
            if r == 0:
                rolled[r, e] = padded[e]
            else:
                rolled[r, e, 0:40] = padded[e, r:r + 40, :]

    def step(v, best):
        total = jnp.zeros((BAND, PADW), f32)
        for e in range(EPOCHS):
            down = SMAX + shifts[v * 16 + 2 * e]
            across = shifts[v * 16 + 2 * e + 1]
            first = pl.multiple_of((down // 8) * 8, 8)
            window = rolled[down % 8, e, pl.ds(first, BAND), :]
            amount = jnp.where(across > 0, PADW - across, -across)
            total = total + pltpu.roll(window, amount, 1)
        return jnp.maximum(best, total[:, 0:W])

    best = lax.fori_loop(0, count[0], step, jnp.full((BAND, W), -1e30, f32))
    out[...] = best / scale[0]


def vmem():
    return pl.BlockSpec(memory_space=pltpu.VMEM)


def smem():
    return pl.BlockSpec(memory_space=pltpu.SMEM)


def on_device(visits, template, basis_taps, coeffs, psf_taps, inv_var, shifts, vel_count):
    visits, inv_var, psf = visits[0], inv_var[0], psf_taps[0]
    tiles = lax.axis_size("sky")
    epochs = lax.axis_size("epoch")
    epoch = lax.axis_index("epoch")
    own = jnp.pad(coeffs[0, 0].T, ((0, 5), (0, 128 - NB)))
    wide = jnp.pad(own, ((0, 0), (0, W - 128)))
    to_below = jnp.concatenate([visits[H - VEDGE:], inv_var[H - SMAX:], wide, template], axis=0)
    to_above = jnp.concatenate([visits[:VEDGE], inv_var[:SMAX], wide, template], axis=0)
    above = lax.ppermute(to_below, "sky", [(i, i + 1) for i in range(tiles - 1)])
    below = lax.ppermute(to_above, "sky", [(i + 1, i) for i in range(tiles - 1)])
    power = jnp.sum(psf * psf)
    weight = power * power * jnp.mean(inv_var)
    extra = jnp.where(epoch < 4, below[48:64], above[48:64])
    block = jnp.concatenate([template, extra, jnp.broadcast_to(weight, (8, W))], axis=0)
    bands = lax.all_to_all(jnp.broadcast_to(block[None], (epochs, 40, W)), "epoch", 0, 0, tiled=True)
    scale = jnp.sqrt(jnp.sum(bands[:, 32, 0]))[None]
    col_taps = jnp.pad(basis_taps[1].T, ((0, 24 - TAPS), (0, 128 - NB)))
    row_taps = jnp.pad(basis_taps[0], ((0, 128 - NB), (0, 128 - TAPS)))
    windows = pl.pallas_call(
        filter_kernel,
        out_shape=jax.ShapeDtypeStruct((EPOCHS, 3 * BAND, W), bf16),
        in_specs=[smem()] + [vmem()] * 8,
        out_specs=vmem(),
        scratch_shapes=[
            pltpu.VMEM((TAPS, EXT, W), bf16),
            pltpu.VMEM((TAPS, EXT, W), bf16),
            pltpu.VMEM((2, 2 * HALF, TAPS * WIN), bf16),
            pltpu.VMEM((2, 2 * HALF, TAPS * WIN), bf16),
            pltpu.VMEM((2 * HALF, W), f32),
        ],
        name="filter",
    )(psf, visits, inv_var, above, below, bands, own, col_taps, row_taps)
    moved = lax.all_to_all(windows, "epoch", 0, 0, tiled=True)
    return pl.pallas_call(
        search_kernel,
        out_shape=jax.ShapeDtypeStruct((BAND, W), f32),
        in_specs=[smem(), smem(), smem(), vmem()],
        out_specs=vmem(),
        scratch_shapes=[
            pltpu.VMEM((EPOCHS, 3 * BAND, PADW), f32),
            pltpu.VMEM((8, EPOCHS, 3 * BAND, PADW), f32),
        ],
        name="search",
    )(vel_count, shifts.reshape(-1), scale, moved)


def solution(mesh):
    in_specs = (
        P("epoch", "sky", None),
        P(("sky", "epoch"), None),
        P(),
        P("epoch", "sky", None, None),
        P("epoch", None),
        P("epoch", "sky", None),
        P("sky", None, None, None),
        P("sky"),
    )
    out_specs = P(("sky", "epoch"), None)
    return jax.shard_map(
        on_device, mesh=mesh, in_specs=in_specs, out_specs=out_specs, check_vma=False
    )
```

```python
import jax
import jax.numpy as jnp
from jax import lax
from jax.experimental import pallas as pl
from jax.experimental.pallas import tpu as pltpu
from jax.sharding import PartitionSpec as P

NB = 27
R = 8
F = 4
SMAX = 16
EPOCHS = 8
H = 128
W = 1024
BAND = 16
TAPS = 2 * R + 1
PTAPS = 2 * F + 1
VEDGE = 24
TEDGE = 32
MID = 56
MWIN = 80
EDGE = 32
EWIN = 48
NBLK = 256
PADW = W + 128
OUTR = 56
DROWS = 2 * EDGE + 2 * MID
FROWS = H + 2 * SMAX
MIDDLE = (H - 1) / 2.0
f32 = jnp.float32
bf16 = jnp.bfloat16


def toeplitz(coeff_rows, col_taps, row_taps, table):
    scaled = [col_taps * rows[p:p + 1, :] for rows in coeff_rows for p in range(3)]
    profiles = jnp.dot(jnp.concatenate(scaled, axis=0), row_taps,
                       precision=lax.Precision.HIGHEST, preferred_element_type=f32)
    for s in range(8):
        moved = profiles if s == 0 else pltpu.roll(profiles, s, 1)
        for i in range(len(scaled)):
            table[i, pl.ds(s, 24, stride=8), :] = moved[24 * i:24 * i + 24]


def band_rows(table, at, window, offset, first_row, lanes, store):
    lane = lax.broadcasted_iota(jnp.int32, (8, 128), 1)
    row = lax.broadcasted_iota(jnp.int32, (8, 128), 0) + first_row
    w = (row.astype(f32) - MIDDLE) / MIDDLE
    for q in range((lanes + 127) // 128):
        even, odd = jnp.zeros((8, 128), f32), jnp.zeros((8, 128), f32)
        for l in range(TAPS):
            a = l * window + offset
            low = a % 128
            if a // 128 == q:
                keep = None if low + 24 <= 128 else lane >= low
            elif (a + 23) // 128 == q:
                keep = lane < 24
            else:
                continue
            parts = []
            for p in range(3):
                piece = table[at + p, 8 * l:8 * l + 8, :]
                if low:
                    piece = pltpu.roll(piece, low, 1)
                if keep is not None:
                    piece = jnp.where(keep, piece, 0.0)
                parts.append(piece)
            even = even + (parts[0] + w * parts[2])
            odd = odd + parts[1]
        store(q, even, odd)


def split(x):
    hi = x.astype(bf16)
    return hi, (x - hi.astype(f32)).astype(bf16)


def shift_band(band, hi_ref, lo_ref, at):
    blank = jnp.zeros((BAND, PADW - W), bf16)
    for piece, ref in zip(split(band), (hi_ref, lo_ref)):
        piece = jnp.concatenate([piece, blank], axis=1)
        for l in range(TAPS):
            moved = piece if l == R else pltpu.roll(piece, (R - l) % PADW, 1)
            ref[l, at:at + BAND, :] = moved[:, 0:W]


def model_block(lhs, hi_ref, lo_ref, rows, count, n):
    cols = slice(n * NBLK, (n + 1) * NBLK)
    depth = TAPS * (rows.stop - rows.start)
    acc = jnp.dot(lhs, hi_ref[:, rows, cols].reshape(depth, NBLK), preferred_element_type=f32)
    acc = acc[0:2 * count] + acc[2 * count:4 * count] + jnp.dot(
        lhs[0:2 * count], lo_ref[:, rows, cols].reshape(depth, NBLK), preferred_element_type=f32)
    col = lax.broadcasted_iota(jnp.int32, (count, NBLK), 1) + n * NBLK
    u = (col.astype(f32) - (W - 1) / 2.0) / ((W - 1) / 2.0)
    return acc[0:count] + u * acc[count:2 * count]


def row_filter(psf, lhs, wide):
    lane = lax.broadcasted_iota(jnp.int32, (8, 128), 1)
    sub = lax.broadcasted_iota(jnp.int32, (8, 128), 0)
    taps = jnp.zeros((8, 128), f32)
    for k in range(PTAPS):
        taps = jnp.where(lane - sub == k, psf[k], taps)
    for g in range(FROWS // 8):
        low = (8 * g + 4) % 128
        moved = pltpu.roll(taps, low, 1)
        first, second = (8 * g + 4) // 128, (8 * g + 19) // 128
        pieces = [jnp.zeros((8, 128), f32)] * 2
        if first == second:
            pieces[first] = moved
        else:
            pieces[first] = jnp.where(lane >= low, moved, 0.0)
            pieces[second] = jnp.where(lane < low, moved, 0.0)
        wide[8 * g:8 * g + 8, 0:128] = pieces[0]
        wide[8 * g:8 * g + 8, 128:DROWS] = pieces[1][:, 0:DROWS - 128]
    hi, lo = split(wide[...])
    lhs[0:FROWS, :] = hi
    lhs[FROWS:2 * FROWS, :] = lo


def prepare_kernel(psf, inv_var, coeffs, col_taps, row_taps, lhs, weight, smoother, table, wide, psf_wide):
    row_filter(psf, smoother, psf_wide)
    toeplitz([coeffs[...]], col_taps[...], row_taps[...], table)
    lanes = TAPS * MWIN
    for block in range(2):
        for g in range(MID // 8):
            def store(q, even, odd, block=block, g=g):
                end = min(128, lanes - q * 128)
                wide[block, 8 * g:8 * g + 8, q * 128:q * 128 + end] = even[:, 0:end]
                wide[block, MID + 8 * g:MID + 8 * g + 8, q * 128:q * 128 + end] = odd[:, 0:end]
            band_rows(table, 0, MWIN, 8 * g + 8 * block, 8 + MID * block + 8 * g, lanes, store)
        hi, lo = split(wide[block])
        lhs[block, 0:2 * MID, :] = hi
        lhs[block, 2 * MID:4 * MID, :] = lo
    power = psf[0] * psf[0]
    for k in range(1, PTAPS):
        power = power + psf[k] * psf[k]
    weight[...] = jnp.full((8, 128), power * power * (jnp.sum(inv_var[...]) / (H * W)), f32)


def inner_kernel(bands, lhs, visits, diff, hi_ref, lo_ref):
    for e in range(EPOCHS):
        shift_band(bands[e], hi_ref, lo_ref, e * BAND)
    for block in range(2):
        rows = slice(0, MWIN) if block == 0 else slice(H - MWIN, H)
        for n in range(W // NBLK):
            cols = slice(n * NBLK, (n + 1) * NBLK)
            model = model_block(lhs[block], hi_ref, lo_ref, rows, MID, n)
            diff[MID * block:MID * (block + 1), cols] = visits[8 + MID * block:8 + MID * (block + 1), cols] - model


def outer_kernel(psf, visits, inv_var, above, below, bands, inner, coeffs, col_taps, row_taps, weight, smoother,
                 out, table, wide, lhs, hi_ref, lo_ref, diff, smoothed):
    toeplitz([above[40:48, 0:128], coeffs[...], below[40:48, 0:128]], col_taps[...], row_taps[...], table)
    lanes = TAPS * EWIN
    for block in range(2):
        for g in range(4):
            if block == 0:
                at, first = (0, H - VEDGE + 8 * g) if g < 3 else (3, 0)
            else:
                at, first = (6, 8 * (g - 1)) if g > 0 else (3, H - 8)

            def store(q, even, odd, block=block, g=g):
                end = min(128, lanes - q * 128)
                wide[block, 8 * g:8 * g + 8, q * 128:q * 128 + end] = even[:, 0:end]
                wide[block, EDGE + 8 * g:EDGE + 8 * g + 8, q * 128:q * 128 + end] = odd[:, 0:end]
            band_rows(table, at, EWIN, 8 * g, first, lanes, store)
        hi, lo = split(wide[block])
        lhs[block, 0:2 * EDGE, :] = hi
        lhs[block, 2 * EDGE:4 * EDGE, :] = lo
    shift_band(above[48:64, :], hi_ref, lo_ref, 0)
    shift_band(above[64:80, :], hi_ref, lo_ref, 16)
    shift_band(bands[0], hi_ref, lo_ref, 32)
    shift_band(bands[EPOCHS - 1], hi_ref, lo_ref, 48)
    shift_band(below[48:64, :], hi_ref, lo_ref, 64)
    shift_band(below[64:80, :], hi_ref, lo_ref, 80)
    diff[EDGE:EDGE + 2 * MID, :] = inner[...]
    low = EDGE + 2 * MID
    for n in range(W // NBLK):
        cols = slice(n * NBLK, (n + 1) * NBLK)
        model = model_block(lhs[0], hi_ref, lo_ref, slice(0, EWIN), EDGE, n)
        diff[0:VEDGE, cols] = above[0:VEDGE, cols] - model[0:VEDGE]
        diff[VEDGE:EDGE, cols] = visits[0:8, cols] - model[VEDGE:EDGE]
        model = model_block(lhs[1], hi_ref, lo_ref, slice(EWIN, 2 * EWIN), EDGE, n)
        diff[low:low + 8, cols] = visits[H - 8:H, cols] - model[0:8]
        diff[low + 8:low + EDGE, cols] = below[0:VEDGE, cols] - model[8:EDGE]

    smoothed[:, W:PADW] = jnp.zeros((FROWS, PADW - W), f32)
    for n in range(W // NBLK):
        cols = slice(n * NBLK, (n + 1) * NBLK)
        hi, lo = split(diff[:, cols])
        both = jnp.dot(smoother[...], hi, preferred_element_type=f32)
        smoothed[:, cols] = both[0:FROWS] + both[FROWS:2 * FROWS] + jnp.dot(
            smoother[0:FROWS, :], lo, preferred_element_type=f32)
    for c in range(10):
        smooth = smoothed[16 * c:16 * c + 16, :]
        total = psf[F] * smooth
        for k in range(PTAPS):
            if k != F:
                total = total + psf[k] * pltpu.roll(smooth, (F - k) % PADW, 1)
        total = total[:, 0:W]
        if c == 0:
            scale = above[24:40, :]
        elif c == 9:
            scale = below[24:40, :]
        else:
            scale = inv_var[16 * (c - 1):16 * c, :]
        rounded = (total * scale).astype(bf16)
        for part in range(3):
            owner = c - part
            if 0 <= owner < EPOCHS:
                out[owner, part * 16:(part + 1) * 16, :] = rounded
    first = weight[...].astype(bf16)
    rest = weight[...] - first.astype(f32)
    second = rest.astype(bf16)
    third = (rest - second.astype(f32)).astype(bf16)
    last = jnp.concatenate([first, second, third, jnp.zeros((8, W - 384), bf16)], axis=1)
    for owner in range(EPOCHS):
        out[owner, 48:OUTR, :] = last


def search_kernel(count, shifts, windows, out, table):
    weight_sum = jnp.zeros((8, 128), f32)
    for e in range(EPOCHS):
        rows = windows[e, 0:48, :].astype(f32)
        for q in range(8):
            table[e, pl.ds(q, 48, stride=8), :] = rows[:, q * 128:(q + 1) * 128]
        for q in range(3):
            weight_sum = weight_sum + windows[e, 48:OUTR, q * 128:(q + 1) * 128].astype(f32)
    lane = lax.broadcasted_iota(jnp.int32, (8, 128), 1)
    sub = lax.broadcasted_iota(jnp.int32, (8, 128), 0)
    right = (lane >= 64)[None]
    from_next = ((lane >= 64) & (sub < 7))[None]
    from_last = ((lane < 64) & (sub > 0))[None]

    def stack(v, half):
        whole = jnp.zeros((8, 8, 128), f32)
        inside = jnp.zeros((8, 8, 128), f32)
        for e in range(EPOCHS):
            down = shifts[v * 16 + 2 * e]
            across = shifts[v * 16 + 2 * e + 1]
            first = pl.multiple_of((SMAX + 8 * half + down) * 8, 8)
            window = table[e, pl.ds(first, 64), :]
            moved = pltpu.roll(window, (128 - across) % 128, 1).reshape(8, 8, 128)
            source = lane + across
            keep = ((source >= 0) & (source < 128))[None]
            whole = whole + moved
            inside = inside + jnp.where(keep, moved, 0.0)
        outside = whole - inside
        total = inside + jnp.where(from_next, pltpu.roll(outside, 7, 1), 0.0)
        return total + jnp.where(from_last, pltpu.roll(outside, 1, 1), 0.0)

    most = count[0] - 1

    def step(turn, best):
        first, second = 2 * turn, jnp.minimum(2 * turn + 1, most)
        tops = jnp.maximum(best[0], jnp.maximum(stack(first, 0), stack(second, 0)))
        lows = jnp.maximum(best[1], jnp.maximum(stack(first, 1), stack(second, 1)))
        return tops, lows

    least = jnp.full((8, 8, 128), -1e30, f32)
    best = lax.fori_loop(0, (count[0] + 1) // 2, step, (least, least))
    norm = jnp.sqrt(weight_sum)[None]
    for half in range(2):
        table[0, half * 64:half * 64 + 64, :] = (best[half] / norm).reshape(64, 128)
    for q in range(8):
        out[:, q * 128:(q + 1) * 128] = table[0, pl.ds(q, BAND, stride=8), :]


def vmem(count):
    return [pl.BlockSpec(memory_space=pltpu.VMEM)] * count


def smem(count):
    return [pl.BlockSpec(memory_space=pltpu.SMEM)] * count


def shape(*dims, dtype=f32):
    return jax.ShapeDtypeStruct(dims, dtype)


def held(x):
    return pltpu.with_memory_space_constraint(x, pltpu.VMEM)


def on_device(visits, template, basis_taps, coeffs, psf_taps, inv_var, shifts, vel_count):
    visits, inv_var, psf = visits[0], inv_var[0], psf_taps[0]
    tiles = lax.axis_size("sky")
    epochs = lax.axis_size("epoch")
    bands = lax.all_to_all(jnp.broadcast_to(template[None], (epochs, BAND, W)), "epoch", 0, 0, tiled=True)
    own = jnp.pad(coeffs[0, 0].T, ((0, 5), (0, 128 - NB)))
    wide = jnp.pad(own, ((0, 0), (0, W - 128)))
    col_taps = jnp.pad(basis_taps[1].T, ((0, 24 - TAPS), (0, 128 - NB)))
    row_taps = jnp.pad(basis_taps[0], ((0, 128 - NB), (0, 128 - TAPS)))
    lhs, weight, smoother = pl.pallas_call(
        prepare_kernel,
        out_shape=(
            pltpu.VMEM((2, 4 * MID, TAPS * MWIN), bf16),
            shape(8, 128),
            pltpu.VMEM((2 * FROWS, DROWS), bf16),
        ),
        in_specs=smem(1) + vmem(4),
        out_specs=tuple(vmem(3)),
        scratch_shapes=[
            pltpu.VMEM((3, 192, 128), f32),
            pltpu.VMEM((2, 2 * MID, TAPS * MWIN), f32),
            pltpu.VMEM((FROWS, DROWS), f32),
        ],
        compiler_params=pltpu.CompilerParams(vmem_limit_bytes=8 << 20),
        name="prepare",
    )(psf, held(inv_var), held(own), held(col_taps), held(row_taps))
    bands, weight = lax.optimization_barrier((bands, weight))
    to_below = jnp.concatenate([visits[H - VEDGE:], inv_var[H - SMAX:], wide, bands[6:].reshape(TEDGE, W)], axis=0)
    to_above = jnp.concatenate([visits[:VEDGE], inv_var[:SMAX], wide, bands[:2].reshape(TEDGE, W)], axis=0)
    above = lax.ppermute(to_below, "sky", [(i, i + 1) for i in range(tiles - 1)])
    below = lax.ppermute(to_above, "sky", [(i + 1, i) for i in range(tiles - 1)])
    inner = pl.pallas_call(
        inner_kernel,
        out_shape=pltpu.VMEM((2 * MID, W), f32),
        in_specs=vmem(3),
        out_specs=vmem(1)[0],
        scratch_shapes=[pltpu.VMEM((TAPS, H, W), bf16), pltpu.VMEM((TAPS, H, W), bf16)],
        compiler_params=pltpu.CompilerParams(vmem_limit_bytes=24 << 20),
        name="inner",
    )(held(bands), lhs, held(visits))
    windows = pl.pallas_call(
        outer_kernel,
        out_shape=shape(EPOCHS, OUTR, W, dtype=bf16),
        in_specs=smem(1) + vmem(11),
        out_specs=vmem(1)[0],
        scratch_shapes=[
            pltpu.VMEM((9, 192, 128), f32),
            pltpu.VMEM((2, 2 * EDGE, TAPS * EWIN), f32),
            pltpu.VMEM((2, 4 * EDGE, TAPS * EWIN), bf16),
            pltpu.VMEM((TAPS, 2 * EWIN, W), bf16),
            pltpu.VMEM((TAPS, 2 * EWIN, W), bf16),
            pltpu.VMEM((DROWS, W), f32),
            pltpu.VMEM((FROWS, PADW), f32),
        ],
        compiler_params=pltpu.CompilerParams(vmem_limit_bytes=24 << 20),
        name="outer",
    )(psf, held(visits), held(inv_var), held(above), held(below), held(bands), inner, held(own), held(col_taps), held(row_taps),
      held(weight), smoother)
    moved = lax.all_to_all(windows, "epoch", 0, 0, tiled=True)
    return pl.pallas_call(
        search_kernel,
        out_shape=shape(BAND, W),
        in_specs=smem(2) + vmem(1),
        out_specs=vmem(1)[0],
        scratch_shapes=[pltpu.VMEM((EPOCHS, 384, 128), f32)],
        compiler_params=pltpu.CompilerParams(vmem_limit_bytes=8 << 20),
        name="search",
    )(vel_count, shifts.reshape(-1), held(moved))


def solution(mesh):
    in_specs = (
        P("epoch", "sky", None),
        P(("sky", "epoch"), None),
        P(),
        P("epoch", "sky", None, None),
        P("epoch", None),
        P("epoch", "sky", None),
        P("sky", None, None, None),
        P("sky"),
    )
    out_specs = P(("sky", "epoch"), None)
    return jax.shard_map(
        on_device, mesh=mesh, in_specs=in_specs, out_specs=out_specs, check_vma=False
    )
```

```python
import jax
import jax.numpy as jnp
from jax import lax
from jax.experimental import pallas as pl
from jax.experimental.pallas import tpu as pltpu
from jax.sharding import PartitionSpec as P

NB = 27
R = 8
F = 4
SMAX = 16
EPOCHS = 8
H = 128
W = 1024
BAND = 16
TAPS = 2 * R + 1
PTAPS = 2 * F + 1
VEDGE = 24
TEDGE = 32
MID = 56
MWIN = 80
EDGE = 32
EWIN = 48
NBLK = 256
PADW = W + 128
OUTR = 56
IROWS = H - 2 * BAND
OROWS = 2 * BAND
CWIN = 2 * NBLK
MIDDLE = (H - 1) / 2.0
f32 = jnp.float32
bf16 = jnp.bfloat16


def toeplitz(coeff_rows, col_taps, row_taps, table):
    scaled = [col_taps * rows[p:p + 1, :] for rows in coeff_rows for p in range(3)]
    profiles = jnp.dot(jnp.concatenate(scaled, axis=0), row_taps,
                       precision=lax.Precision.HIGHEST, preferred_element_type=f32)
    for s in range(8):
        moved = profiles if s == 0 else pltpu.roll(profiles, s, 1)
        for i in range(len(scaled)):
            table[i, pl.ds(s, 24, stride=8), :] = moved[24 * i:24 * i + 24]


def band_rows(table, at, window, offset, first_row, lanes, store):
    lane = lax.broadcasted_iota(jnp.int32, (8, 128), 1)
    row = lax.broadcasted_iota(jnp.int32, (8, 128), 0) + first_row
    w = (row.astype(f32) - MIDDLE) / MIDDLE
    for q in range((lanes + 127) // 128):
        even, odd = jnp.zeros((8, 128), f32), jnp.zeros((8, 128), f32)
        for l in range(TAPS):
            a = l * window + offset
            low = a % 128
            if a // 128 == q:
                keep = None if low + 24 <= 128 else lane >= low
            elif (a + 23) // 128 == q:
                keep = lane < 24
            else:
                continue
            parts = []
            for p in range(3):
                piece = table[at + p, 8 * l:8 * l + 8, :]
                if low:
                    piece = pltpu.roll(piece, low, 1)
                if keep is not None:
                    piece = jnp.where(keep, piece, 0.0)
                parts.append(piece)
            even = even + (parts[0] + w * parts[2])
            odd = odd + parts[1]
        store(q, even, odd)


def split(x):
    hi = x.astype(bf16)
    return hi, (x - hi.astype(f32)).astype(bf16)


def shift_band(band, hi_ref, lo_ref, at, copies=None, copy_at=0):
    blank = jnp.zeros((BAND, PADW - W), bf16)
    for i, (piece, ref) in enumerate(zip(split(band), (hi_ref, lo_ref))):
        piece = jnp.concatenate([piece, blank], axis=1)
        for l in range(TAPS):
            moved = piece if l == R else pltpu.roll(piece, (R - l) % PADW, 1)
            ref[l, at:at + BAND, :] = moved[:, 0:W]
            if copies:
                copies[i][l, copy_at:copy_at + BAND, :] = moved[:, 0:W]


def model_block(lhs, hi_ref, lo_ref, rows, count, n):
    cols = slice(n * NBLK, (n + 1) * NBLK)
    depth = TAPS * (rows.stop - rows.start)
    acc = jnp.dot(lhs, hi_ref[:, rows, cols].reshape(depth, NBLK), preferred_element_type=f32)
    acc = acc[0:2 * count] + acc[2 * count:4 * count] + jnp.dot(
        lhs[0:2 * count], lo_ref[:, rows, cols].reshape(depth, NBLK), preferred_element_type=f32)
    col = lax.broadcasted_iota(jnp.int32, (count, NBLK), 1) + n * NBLK
    u = (col.astype(f32) - (W - 1) / 2.0) / ((W - 1) / 2.0)
    return acc[0:count] + u * acc[count:2 * count]


def filter_matrices(psf, inner_rows, outer_rows, cols, wide):
    lane = lax.broadcasted_iota(jnp.int32, (8, 128), 1)
    sub = lax.broadcasted_iota(jnp.int32, (8, 128), 0)
    taps = jnp.zeros((8, 128), f32)
    for k in range(PTAPS):
        taps = jnp.where(lane - sub == k, psf[k], taps)
    for g in range(IROWS // 8):
        wide[8 * g:8 * g + 8, :] = pltpu.roll(taps, 8 * g + 4, 1)[:, 0:2 * MID]
    for rows, depth, ref in ((IROWS, 2 * MID, inner_rows), (OROWS, EWIN, outer_rows)):
        hi, lo = split(wide[0:rows, 0:depth])
        ref[0:rows, :] = hi
        ref[rows:2 * rows, :] = lo
    for at in range(0, CWIN, 128):
        offset = lax.broadcasted_iota(jnp.int32, (128, NBLK), 0) - lax.broadcasted_iota(jnp.int32, (128, NBLK), 1) + (at - 124)
        block = jnp.zeros((128, NBLK), f32)
        for k in range(PTAPS):
            block = jnp.where(offset == k, psf[k], block)
        hi, lo = split(block)
        cols[0, at:at + 128, :] = hi
        cols[1, at:at + 128, :] = lo


def filter_cols(count, halves, col_filter, store):
    for n in range(W // NBLK):
        window = slice(n * NBLK, n * NBLK + CWIN)
        acc = jnp.dot(halves[:, window], col_filter[0], preferred_element_type=f32)
        acc = acc[0:count] + acc[count:2 * count] + jnp.dot(
            halves[0:count, window], col_filter[1], preferred_element_type=f32)
        store(slice(n * NBLK, (n + 1) * NBLK), acc)


def filter_rows(count, matrix, rows):
    hi, lo = split(rows)
    acc = jnp.dot(matrix[...], hi, preferred_element_type=f32)
    return acc[0:count] + acc[count:2 * count] + jnp.dot(matrix[0:count, :], lo, preferred_element_type=f32)


def clear_margins(halves):
    blank = jnp.zeros((halves.shape[0], 128), bf16)
    halves[:, 0:128] = blank
    halves[:, W + 128:W + 256] = blank


def prepare_kernel(psf, inv_var, coeffs, col_taps, row_taps, lhs, weight, inner_rows, outer_rows, cols,
                   table, wide, psf_wide):
    filter_matrices(psf, inner_rows, outer_rows, cols, psf_wide)
    toeplitz([coeffs[...]], col_taps[...], row_taps[...], table)
    lanes = TAPS * MWIN
    for block in range(2):
        for g in range(MID // 8):
            def store(q, even, odd, block=block, g=g):
                end = min(128, lanes - q * 128)
                wide[block, 8 * g:8 * g + 8, q * 128:q * 128 + end] = even[:, 0:end]
                wide[block, MID + 8 * g:MID + 8 * g + 8, q * 128:q * 128 + end] = odd[:, 0:end]
            band_rows(table, 0, MWIN, 8 * g + 8 * block, 8 + MID * block + 8 * g, lanes, store)
        hi, lo = split(wide[block])
        lhs[block, 0:2 * MID, :] = hi
        lhs[block, 2 * MID:4 * MID, :] = lo
    power = psf[0] * psf[0]
    for k in range(1, PTAPS):
        power = power + psf[k] * psf[k]
    weight[...] = jnp.full((8, 128), power * power * (jnp.sum(inv_var[...]) / (H * W)), f32)


def inner_kernel(bands, lhs, visits, inv_var, row_filter, col_filter,
                 filtered, diff_edges, hi_edges, lo_edges, hi_ref, lo_ref, diff, halves):
    for e in range(EPOCHS):
        copies = None if 0 < e < EPOCHS - 1 else (hi_edges, lo_edges)
        shift_band(bands[e], hi_ref, lo_ref, e * BAND, copies, 0 if e == 0 else BAND)
    clear_margins(halves)
    for n in range(W // NBLK):
        cols = slice(n * NBLK, (n + 1) * NBLK)
        for block in range(2):
            rows = slice(0, MWIN) if block == 0 else slice(H - MWIN, H)
            model = model_block(lhs[block], hi_ref, lo_ref, rows, MID, n)
            diff[MID * block:MID * (block + 1), cols] = visits[8 + MID * block:8 + MID * (block + 1), cols] - model
        hi, lo = split(filter_rows(IROWS, row_filter, diff[:, cols]))
        halves[0:IROWS, 128 + n * NBLK:128 + (n + 1) * NBLK] = hi
        halves[IROWS:2 * IROWS, 128 + n * NBLK:128 + (n + 1) * NBLK] = lo
    diff_edges[0:BAND, :] = diff[0:BAND, :]
    diff_edges[BAND:2 * BAND, :] = diff[2 * MID - BAND:2 * MID, :]

    def store(cols, values):
        filtered[:, cols] = (values * inv_var[BAND:H - BAND, cols]).astype(bf16)
    filter_cols(IROWS, halves, col_filter, store)


def outer_kernel(visits, inv_var, above, below, t_above, t_below, filtered, diff_edges, hi_edges, lo_edges, coeffs,
                 col_taps, row_taps, weight, row_filter, col_filter,
                 out, table, wide, lhs, hi_ref, lo_ref, diff, halves, ends, last, sems):
    first = weight[...].astype(bf16)
    rest = weight[...] - first.astype(f32)
    second = rest.astype(bf16)
    third = (rest - second.astype(f32)).astype(bf16)
    last[...] = jnp.concatenate([first, second, third, jnp.zeros((8, W - 384), bf16)], axis=1)
    early, late = [], []
    for owner in range(EPOCHS):
        for part in range(3):
            chunk = owner + part
            inside = 2 <= chunk < 8
            source = filtered.at[16 * (chunk - 2):16 * (chunk - 1), :] if inside else ends.at[(0, 1, 8, 9).index(chunk)]
            copy = pltpu.make_async_copy(source, out.at[owner, part * 16:(part + 1) * 16, :], sems.at[owner * 4 + part])
            (early if inside else late).append(copy)
        early.append(pltpu.make_async_copy(last, out.at[owner, 48:OUTR, :], sems.at[owner * 4 + 3]))
    for copy in early:
        copy.start()
    toeplitz([above[40:48, 0:128], coeffs[...], below[40:48, 0:128]], col_taps[...], row_taps[...], table)
    lanes = TAPS * EWIN
    for block in range(2):
        for g in range(4):
            if block == 0:
                at, first = (0, H - VEDGE + 8 * g) if g < 3 else (3, 0)
            else:
                at, first = (6, 8 * (g - 1)) if g > 0 else (3, H - 8)

            def store(q, even, odd, block=block, g=g):
                end = min(128, lanes - q * 128)
                wide[block, 8 * g:8 * g + 8, q * 128:q * 128 + end] = even[:, 0:end]
                wide[block, EDGE + 8 * g:EDGE + 8 * g + 8, q * 128:q * 128 + end] = odd[:, 0:end]
            band_rows(table, at, EWIN, 8 * g, first, lanes, store)
        hi, lo = split(wide[block])
        lhs[block, 0:2 * EDGE, :] = hi
        lhs[block, 2 * EDGE:4 * EDGE, :] = lo
    for edges, ref in ((hi_edges, hi_ref), (lo_edges, lo_ref)):
        for l in range(TAPS):
            ref[l, 32:64, :] = edges[l]
    shift_band(t_above[0:16, :], hi_ref, lo_ref, 0)
    shift_band(t_above[16:32, :], hi_ref, lo_ref, 16)
    shift_band(t_below[0:16, :], hi_ref, lo_ref, 64)
    shift_band(t_below[16:32, :], hi_ref, lo_ref, 80)
    clear_margins(halves)
    diff[0, EDGE:EWIN, :] = diff_edges[0:BAND, :]
    diff[1, 0:BAND, :] = diff_edges[BAND:2 * BAND, :]
    for n in range(W // NBLK):
        cols = slice(n * NBLK, (n + 1) * NBLK)
        model = model_block(lhs[0], hi_ref, lo_ref, slice(0, EWIN), EDGE, n)
        diff[0, 0:VEDGE, cols] = above[0:VEDGE, cols] - model[0:VEDGE]
        diff[0, VEDGE:EDGE, cols] = visits[0:8, cols] - model[VEDGE:EDGE]
        model = model_block(lhs[1], hi_ref, lo_ref, slice(EWIN, 2 * EWIN), EDGE, n)
        diff[1, BAND:BAND + 8, cols] = visits[H - 8:H, cols] - model[0:8]
        diff[1, BAND + 8:EWIN, cols] = below[0:VEDGE, cols] - model[8:EDGE]
        for end in range(2):
            hi, lo = split(filter_rows(OROWS, row_filter, diff[end, :, cols]))
            halves[OROWS * end:OROWS * end + OROWS, 128 + n * NBLK:128 + (n + 1) * NBLK] = hi
            halves[OROWS * (2 + end):OROWS * (3 + end), 128 + n * NBLK:128 + (n + 1) * NBLK] = lo

    def store(cols, values):
        scales = (above[24:40, cols], inv_var[0:BAND, cols], inv_var[H - BAND:H, cols], below[24:40, cols])
        for i in range(4):
            ends[i, :, cols] = (values[16 * i:16 * i + 16] * scales[i]).astype(bf16)
    filter_cols(2 * OROWS, halves, col_filter, store)
    for copy in late:
        copy.start()
    for copy in early + late:
        copy.wait()


def search_kernel(count, starts, across_of, windows, out, table, packed):
    weight_sum = jnp.zeros((8, 128), f32)
    for e in range(EPOCHS):
        rows = windows[e, 0:48, :].astype(f32)
        for q in range(8):
            table[e, pl.ds(q, 48, stride=8), :] = rows[:, q * 128:(q + 1) * 128]
        packed[768 * e:768 * e + 384, :] = table[e].astype(bf16)
        packed[768 * e + 384:768 * e + 752, :] = table[e, 8:376, :].astype(bf16)
        for q in range(3):
            weight_sum = weight_sum + windows[e, 48:OUTR, q * 128:(q + 1) * 128].astype(f32)
    lane = lax.broadcasted_iota(jnp.int32, (8, 128), 1)
    sub = lax.broadcasted_iota(jnp.int32, (8, 128), 0)
    right = (lane >= 64)[None]
    from_next = ((lane >= 64) & (sub < 7))[None]
    from_last = ((lane < 64) & (sub > 0))[None]

    def stack(v, half):
        whole = jnp.zeros((8, 8, 128), f32)
        inside = jnp.zeros((8, 8, 128), f32)
        for e in range(EPOCHS):
            across = across_of[v * EPOCHS + e]
            first = pl.multiple_of(starts[v * EPOCHS + e] + 64 * half, 16)
            window = packed[pl.ds(first, 64), :]
            moved = pltpu.roll(window, (-across) & 127, 1).astype(f32).reshape(8, 8, 128)
            source = lane + across
            keep = ((source >= 0) & (source < 128))[None]
            whole = whole + moved
            inside = inside + jnp.where(keep, moved, 0.0)
        outside = whole - inside
        total = inside + jnp.where(from_next, pltpu.roll(outside, 7, 1), 0.0)
        return total + jnp.where(from_last, pltpu.roll(outside, 1, 1), 0.0)

    most = count[0] - 1

    def step(turn, best):
        first, second = 2 * turn, jnp.minimum(2 * turn + 1, most)
        tops = jnp.maximum(best[0], jnp.maximum(stack(first, 0), stack(second, 0)))
        lows = jnp.maximum(best[1], jnp.maximum(stack(first, 1), stack(second, 1)))
        return tops, lows

    least = jnp.full((8, 8, 128), -1e30, f32)
    best = lax.fori_loop(0, (count[0] + 1) // 2, step, (least, least))
    norm = jnp.sqrt(weight_sum)[None]
    for half in range(2):
        table[0, half * 64:half * 64 + 64, :] = (best[half] / norm).reshape(64, 128)
    for q in range(8):
        out[:, q * 128:(q + 1) * 128] = table[0, pl.ds(q, BAND, stride=8), :]


def vmem(count):
    return [pl.BlockSpec(memory_space=pltpu.VMEM)] * count


def smem(count):
    return [pl.BlockSpec(memory_space=pltpu.SMEM)] * count


def shape(*dims, dtype=f32):
    return jax.ShapeDtypeStruct(dims, dtype)


def held(x):
    return pltpu.with_memory_space_constraint(x, pltpu.VMEM)


def to_neighbours(downward, upward):
    tiles = lax.axis_size("sky")
    above = lax.ppermute(downward, "sky", [(i, i + 1) for i in range(tiles - 1)])
    below = lax.ppermute(upward, "sky", [(i + 1, i) for i in range(tiles - 1)])
    return held(above), held(below)


def on_device(visits, template, basis_taps, coeffs, psf_taps, inv_var, shifts, vel_count):
    visits, inv_var, psf = visits[0], inv_var[0], psf_taps[0]
    epochs = lax.axis_size("epoch")
    bands = lax.all_to_all(jnp.broadcast_to(template[None], (epochs, BAND, W)), "epoch", 0, 0, tiled=True)
    own = jnp.pad(coeffs[0, 0].T, ((0, 5), (0, 128 - NB)))
    wide = jnp.pad(own, ((0, 0), (0, W - 128)))
    above, below = to_neighbours(
        jnp.concatenate([visits[H - VEDGE:], inv_var[H - SMAX:], wide], axis=0),
        jnp.concatenate([visits[:VEDGE], inv_var[:SMAX], wide], axis=0),
    )
    col_taps = jnp.pad(basis_taps[1].T, ((0, 24 - TAPS), (0, 128 - NB)))
    row_taps = jnp.pad(basis_taps[0], ((0, 128 - NB), (0, 128 - TAPS)))
    lhs, weight, inner_rows, outer_rows, col_filter = pl.pallas_call(
        prepare_kernel,
        out_shape=(
            pltpu.VMEM((2, 4 * MID, TAPS * MWIN), bf16),
            shape(8, 128),
            pltpu.VMEM((2 * IROWS, 2 * MID), bf16),
            pltpu.VMEM((2 * OROWS, EWIN), bf16),
            pltpu.VMEM((2, CWIN, NBLK), bf16),
        ),
        in_specs=smem(1) + vmem(4),
        out_specs=tuple(vmem(5)),
        scratch_shapes=[
            pltpu.VMEM((3, 192, 128), f32),
            pltpu.VMEM((2, 2 * MID, TAPS * MWIN), f32),
            pltpu.VMEM((IROWS, 2 * MID), f32),
        ],
        compiler_params=pltpu.CompilerParams(vmem_limit_bytes=8 << 20),
        name="prepare",
    )(psf, held(inv_var), held(own), held(col_taps), held(row_taps))
    bands, weight = lax.optimization_barrier((bands, weight))
    t_above, t_below = to_neighbours(bands[6:].reshape(TEDGE, W), bands[:2].reshape(TEDGE, W))
    filtered, diff_edges, hi_edges, lo_edges = pl.pallas_call(
        inner_kernel,
        out_shape=(
            pltpu.VMEM((IROWS, W), bf16),
            pltpu.VMEM((2 * BAND, W), f32),
            pltpu.VMEM((TAPS, 2 * BAND, W), bf16),
            pltpu.VMEM((TAPS, 2 * BAND, W), bf16),
        ),
        in_specs=vmem(6),
        out_specs=tuple(vmem(4)),
        scratch_shapes=[
            pltpu.VMEM((TAPS, H, W), bf16),
            pltpu.VMEM((TAPS, H, W), bf16),
            pltpu.VMEM((2 * MID, W), f32),
            pltpu.VMEM((2 * IROWS, W + 256), bf16),
        ],
        compiler_params=pltpu.CompilerParams(vmem_limit_bytes=24 << 20),
        name="inner",
    )(held(bands), lhs, held(visits), held(inv_var), inner_rows, col_filter)
    windows = pl.pallas_call(
        outer_kernel,
        out_shape=shape(EPOCHS, OUTR, W, dtype=bf16),
        in_specs=vmem(16),
        out_specs=pl.BlockSpec(memory_space=pl.ANY),
        scratch_shapes=[
            pltpu.VMEM((9, 192, 128), f32),
            pltpu.VMEM((2, 2 * EDGE, TAPS * EWIN), f32),
            pltpu.VMEM((2, 4 * EDGE, TAPS * EWIN), bf16),
            pltpu.VMEM((TAPS, 2 * EWIN, W), bf16),
            pltpu.VMEM((TAPS, 2 * EWIN, W), bf16),
            pltpu.VMEM((2, EWIN, W), f32),
            pltpu.VMEM((4 * OROWS, W + 256), bf16),
            pltpu.VMEM((4, BAND, W), bf16),
            pltpu.VMEM((8, W), bf16),
            pltpu.SemaphoreType.DMA((4 * EPOCHS,)),
        ],
        compiler_params=pltpu.CompilerParams(vmem_limit_bytes=24 << 20),
        name="outer",
    )(held(visits), held(inv_var), above, below, t_above, t_below, filtered, diff_edges, hi_edges, lo_edges,
      held(own), held(col_taps), held(row_taps), held(weight), outer_rows, col_filter)
    down = shifts[0, :, :, 0] + SMAX
    starts = jnp.arange(EPOCHS, dtype=jnp.int32) * 768 + (down & 1) * 384 + (down - (down & 1)) * 8
    moved = lax.all_to_all(windows, "epoch", 0, 0, tiled=True)
    return pl.pallas_call(
        search_kernel,
        out_shape=shape(BAND, W),
        in_specs=smem(3) + vmem(1),
        out_specs=vmem(1)[0],
        scratch_shapes=[pltpu.VMEM((EPOCHS, 384, 128), f32), pltpu.VMEM((2 * EPOCHS * 384, 128), bf16)],
        compiler_params=pltpu.CompilerParams(vmem_limit_bytes=12 << 20),
        name="search",
    )(vel_count, starts.reshape(-1), shifts[0, :, :, 1].reshape(-1), held(moved))


def solution(mesh):
    in_specs = (
        P("epoch", "sky", None),
        P(("sky", "epoch"), None),
        P(),
        P("epoch", "sky", None, None),
        P("epoch", None),
        P("epoch", "sky", None),
        P("sky", None, None, None),
        P("sky"),
    )
    out_specs = P(("sky", "epoch"), None)
    return jax.shard_map(
        on_device, mesh=mesh, in_specs=in_specs, out_specs=out_specs, check_vma=False
    )
```

```python
import jax
import jax.numpy as jnp
from jax import lax
from jax.experimental import pallas as pl
from jax.experimental.pallas import tpu as pltpu
from jax.sharding import PartitionSpec as P

NB = 27
R = 8
F = 4
SMAX = 16
EPOCHS = 8
H = 128
W = 1024
BAND = 16
TAPS = 2 * R + 1
PTAPS = 2 * F + 1
VEDGE = 24
TEDGE = 32
MID = 56
MWIN = 80
EDGE = 32
EWIN = 48
NBLK = 256
PADW = W + 128
OUTR = 56
IROWS = H - 2 * BAND
OROWS = 2 * BAND
CWIN = 2 * NBLK
MIDDLE = (H - 1) / 2.0
f32 = jnp.float32
bf16 = jnp.bfloat16


def toeplitz(coeff_rows, col_taps, row_taps, table):
    scaled = [col_taps * rows[p:p + 1, :] for rows in coeff_rows for p in range(3)]
    profiles = jnp.dot(jnp.concatenate(scaled, axis=0), row_taps,
                       precision=lax.Precision.HIGHEST, preferred_element_type=f32)
    for s in range(8):
        moved = profiles if s == 0 else pltpu.roll(profiles, s, 1)
        for i in range(len(scaled)):
            table[i, pl.ds(s, 24, stride=8), :] = moved[24 * i:24 * i + 24]


def band_rows(table, at, window, offset, first_row, lanes, store):
    lane = lax.broadcasted_iota(jnp.int32, (8, 128), 1)
    row = lax.broadcasted_iota(jnp.int32, (8, 128), 0) + first_row
    w = (row.astype(f32) - MIDDLE) / MIDDLE
    for q in range((lanes + 127) // 128):
        even, odd = jnp.zeros((8, 128), f32), jnp.zeros((8, 128), f32)
        for l in range(TAPS):
            a = l * window + offset
            low = a % 128
            if a // 128 == q:
                keep = None if low + 24 <= 128 else lane >= low
            elif (a + 23) // 128 == q:
                keep = lane < 24
            else:
                continue
            parts = []
            for p in range(3):
                piece = table[at + p, 8 * l:8 * l + 8, :]
                if low:
                    piece = pltpu.roll(piece, low, 1)
                if keep is not None:
                    piece = jnp.where(keep, piece, 0.0)
                parts.append(piece)
            even = even + (parts[0] + w * parts[2])
            odd = odd + parts[1]
        store(q, even, odd)


def split(x):
    hi = x.astype(bf16)
    return hi, (x - hi.astype(f32)).astype(bf16)


def shift_band(band, hi_ref, lo_ref, at, copies=None, copy_at=0):
    blank = jnp.zeros((BAND, PADW - W), bf16)
    for i, (piece, ref) in enumerate(zip(split(band), (hi_ref, lo_ref))):
        piece = jnp.concatenate([piece, blank], axis=1)
        for l in range(TAPS):
            moved = piece if l == R else pltpu.roll(piece, (R - l) % PADW, 1)
            ref[l, at:at + BAND, :] = moved[:, 0:W]
            if copies:
                copies[i][l, copy_at:copy_at + BAND, :] = moved[:, 0:W]


def model_block(lhs, hi_ref, lo_ref, rows, count, n):
    cols = slice(n * NBLK, (n + 1) * NBLK)
    depth = TAPS * (rows.stop - rows.start)
    acc = jnp.dot(lhs, hi_ref[:, rows, cols].reshape(depth, NBLK), preferred_element_type=f32)
    acc = acc[0:2 * count] + acc[2 * count:4 * count] + jnp.dot(
        lhs[0:2 * count], lo_ref[:, rows, cols].reshape(depth, NBLK), preferred_element_type=f32)
    col = lax.broadcasted_iota(jnp.int32, (count, NBLK), 1) + n * NBLK
    u = (col.astype(f32) - (W - 1) / 2.0) / ((W - 1) / 2.0)
    return acc[0:count] + u * acc[count:2 * count]


def filter_matrices(psf, inner_rows, outer_rows, cols, wide):
    lane = lax.broadcasted_iota(jnp.int32, (8, 128), 1)
    sub = lax.broadcasted_iota(jnp.int32, (8, 128), 0)
    taps = jnp.zeros((8, 128), f32)
    for k in range(PTAPS):
        taps = jnp.where(lane - sub == k, psf[k], taps)
    for g in range(IROWS // 8):
        wide[8 * g:8 * g + 8, :] = pltpu.roll(taps, 8 * g + 4, 1)[:, 0:2 * MID]
    for rows, depth, ref in ((IROWS, 2 * MID, inner_rows), (OROWS, EWIN, outer_rows)):
        hi, lo = split(wide[0:rows, 0:depth])
        ref[0:rows, :] = hi
        ref[rows:2 * rows, :] = lo
    for at in range(0, CWIN, 128):
        offset = lax.broadcasted_iota(jnp.int32, (128, NBLK), 0) - lax.broadcasted_iota(jnp.int32, (128, NBLK), 1) + (at - 124)
        block = jnp.zeros((128, NBLK), f32)
        for k in range(PTAPS):
            block = jnp.where(offset == k, psf[k], block)
        hi, lo = split(block)
        cols[0, at:at + 128, :] = hi
        cols[1, at:at + 128, :] = lo


def filter_cols(count, halves, col_filter, store):
    for n in range(W // NBLK):
        window = slice(n * NBLK, n * NBLK + CWIN)
        acc = jnp.dot(halves[:, window], col_filter[0], preferred_element_type=f32)
        acc = acc[0:count] + acc[count:2 * count] + jnp.dot(
            halves[0:count, window], col_filter[1], preferred_element_type=f32)
        store(slice(n * NBLK, (n + 1) * NBLK), acc)


def filter_rows(count, matrix, rows):
    hi, lo = split(rows)
    acc = jnp.dot(matrix[...], hi, preferred_element_type=f32)
    return acc[0:count] + acc[count:2 * count] + jnp.dot(matrix[0:count, :], lo, preferred_element_type=f32)


def clear_margins(halves):
    blank = jnp.zeros((halves.shape[0], 128), bf16)
    halves[:, 0:128] = blank
    halves[:, W + 128:W + 256] = blank


def prepare_kernel(psf, inv_var, coeffs, col_taps, row_taps, lhs, weight, inner_rows, outer_rows, cols,
                   table, wide, psf_wide):
    filter_matrices(psf, inner_rows, outer_rows, cols, psf_wide)
    toeplitz([coeffs[...]], col_taps[...], row_taps[...], table)
    lanes = TAPS * MWIN
    for block in range(2):
        for g in range(MID // 8):
            def store(q, even, odd, block=block, g=g):
                end = min(128, lanes - q * 128)
                wide[block, 8 * g:8 * g + 8, q * 128:q * 128 + end] = even[:, 0:end]
                wide[block, MID + 8 * g:MID + 8 * g + 8, q * 128:q * 128 + end] = odd[:, 0:end]
            band_rows(table, 0, MWIN, 8 * g + 8 * block, 8 + MID * block + 8 * g, lanes, store)
        hi, lo = split(wide[block])
        lhs[block, 0:2 * MID, :] = hi
        lhs[block, 2 * MID:4 * MID, :] = lo
    power = psf[0] * psf[0]
    for k in range(1, PTAPS):
        power = power + psf[k] * psf[k]
    weight[...] = jnp.full((8, 128), power * power * (jnp.sum(inv_var[...]) / (H * W)), f32)


def repeat_kernel(band, out, sems):
    copies = [pltpu.make_async_copy(band, out.at[e], sems.at[e]) for e in range(EPOCHS)]
    for copy in copies:
        copy.start()
    for copy in copies:
        copy.wait()


def inner_kernel(bands, lhs, visits, inv_var, row_filter, col_filter,
                 filtered, diff_edges, hi_edges, lo_edges, hi_ref, lo_ref, diff, halves):
    for e in range(EPOCHS):
        copies = None if 0 < e < EPOCHS - 1 else (hi_edges, lo_edges)
        shift_band(bands[e], hi_ref, lo_ref, e * BAND, copies, 0 if e == 0 else BAND)
    clear_margins(halves)
    for n in range(W // NBLK):
        cols = slice(n * NBLK, (n + 1) * NBLK)
        for block in range(2):
            rows = slice(0, MWIN) if block == 0 else slice(H - MWIN, H)
            model = model_block(lhs[block], hi_ref, lo_ref, rows, MID, n)
            diff[MID * block:MID * (block + 1), cols] = visits[8 + MID * block:8 + MID * (block + 1), cols] - model
        hi, lo = split(filter_rows(IROWS, row_filter, diff[:, cols]))
        halves[0:IROWS, 128 + n * NBLK:128 + (n + 1) * NBLK] = hi
        halves[IROWS:2 * IROWS, 128 + n * NBLK:128 + (n + 1) * NBLK] = lo
    diff_edges[0:BAND, :] = diff[0:BAND, :]
    diff_edges[BAND:2 * BAND, :] = diff[2 * MID - BAND:2 * MID, :]

    def store(cols, values):
        filtered[:, cols] = (values * inv_var[BAND:H - BAND, cols]).astype(bf16)
    filter_cols(IROWS, halves, col_filter, store)


def outer_kernel(visits, inv_var, above, below, t_above, t_below, filtered, diff_edges, hi_edges, lo_edges, coeffs,
                 col_taps, row_taps, weight, row_filter, col_filter,
                 out, table, wide, lhs, hi_ref, lo_ref, diff, halves, ends, last, sems):
    first = weight[...].astype(bf16)
    rest = weight[...] - first.astype(f32)
    second = rest.astype(bf16)
    third = (rest - second.astype(f32)).astype(bf16)
    last[...] = jnp.concatenate([first, second, third, jnp.zeros((8, W - 384), bf16)], axis=1)
    early, late = [], []
    for owner in range(EPOCHS):
        for part in range(3):
            chunk = owner + part
            inside = 2 <= chunk < 8
            source = filtered.at[16 * (chunk - 2):16 * (chunk - 1), :] if inside else ends.at[(0, 1, 8, 9).index(chunk)]
            copy = pltpu.make_async_copy(source, out.at[owner, part * 16:(part + 1) * 16, :], sems.at[owner * 4 + part])
            (early if inside else late).append(copy)
        early.append(pltpu.make_async_copy(last, out.at[owner, 48:OUTR, :], sems.at[owner * 4 + 3]))
    for copy in early:
        copy.start()
    toeplitz([above[40:48, 0:128], coeffs[...], below[40:48, 0:128]], col_taps[...], row_taps[...], table)
    lanes = TAPS * EWIN
    for block in range(2):
        for g in range(4):
            if block == 0:
                at, first = (0, H - VEDGE + 8 * g) if g < 3 else (3, 0)
            else:
                at, first = (6, 8 * (g - 1)) if g > 0 else (3, H - 8)

            def store(q, even, odd, block=block, g=g):
                end = min(128, lanes - q * 128)
                wide[block, 8 * g:8 * g + 8, q * 128:q * 128 + end] = even[:, 0:end]
                wide[block, EDGE + 8 * g:EDGE + 8 * g + 8, q * 128:q * 128 + end] = odd[:, 0:end]
            band_rows(table, at, EWIN, 8 * g, first, lanes, store)
        hi, lo = split(wide[block])
        lhs[block, 0:2 * EDGE, :] = hi
        lhs[block, 2 * EDGE:4 * EDGE, :] = lo
    for edges, ref in ((hi_edges, hi_ref), (lo_edges, lo_ref)):
        for l in range(TAPS):
            ref[l, 32:64, :] = edges[l]
    shift_band(t_above[0:16, :], hi_ref, lo_ref, 0)
    shift_band(t_above[16:32, :], hi_ref, lo_ref, 16)
    shift_band(t_below[0:16, :], hi_ref, lo_ref, 64)
    shift_band(t_below[16:32, :], hi_ref, lo_ref, 80)
    clear_margins(halves)
    diff[0, EDGE:EWIN, :] = diff_edges[0:BAND, :]
    diff[1, 0:BAND, :] = diff_edges[BAND:2 * BAND, :]
    for n in range(W // NBLK):
        cols = slice(n * NBLK, (n + 1) * NBLK)
        model = model_block(lhs[0], hi_ref, lo_ref, slice(0, EWIN), EDGE, n)
        diff[0, 0:VEDGE, cols] = above[0:VEDGE, cols] - model[0:VEDGE]
        diff[0, VEDGE:EDGE, cols] = visits[0:8, cols] - model[VEDGE:EDGE]
        model = model_block(lhs[1], hi_ref, lo_ref, slice(EWIN, 2 * EWIN), EDGE, n)
        diff[1, BAND:BAND + 8, cols] = visits[H - 8:H, cols] - model[0:8]
        diff[1, BAND + 8:EWIN, cols] = below[0:VEDGE, cols] - model[8:EDGE]
        for end in range(2):
            hi, lo = split(filter_rows(OROWS, row_filter, diff[end, :, cols]))
            halves[OROWS * end:OROWS * end + OROWS, 128 + n * NBLK:128 + (n + 1) * NBLK] = hi
            halves[OROWS * (2 + end):OROWS * (3 + end), 128 + n * NBLK:128 + (n + 1) * NBLK] = lo

    def store(cols, values):
        scales = (above[24:40, cols], inv_var[0:BAND, cols], inv_var[H - BAND:H, cols], below[24:40, cols])
        for i in range(4):
            ends[i, :, cols] = (values[16 * i:16 * i + 16] * scales[i]).astype(bf16)
    filter_cols(2 * OROWS, halves, col_filter, store)
    for copy in late:
        copy.start()
    for copy in early + late:
        copy.wait()


def search_kernel(count, starts, across_of, windows, out, table, packed):
    weight_sum = jnp.zeros((8, 128), f32)
    for e in range(EPOCHS):
        rows = windows[e, 0:48, :].astype(f32)
        for q in range(8):
            table[e, pl.ds(q, 48, stride=8), :] = rows[:, q * 128:(q + 1) * 128]
        packed[768 * e:768 * e + 384, :] = table[e].astype(bf16)
        packed[768 * e + 384:768 * e + 752, :] = table[e, 8:376, :].astype(bf16)
        for q in range(3):
            weight_sum = weight_sum + windows[e, 48:OUTR, q * 128:(q + 1) * 128].astype(f32)
    lane = lax.broadcasted_iota(jnp.int32, (8, 128), 1)
    sub = lax.broadcasted_iota(jnp.int32, (8, 128), 0)
    right = (lane >= 64)[None]
    from_next = ((lane >= 64) & (sub < 7))[None]
    from_last = ((lane < 64) & (sub > 0))[None]

    def stack(v, half):
        whole = jnp.zeros((8, 8, 128), f32)
        inside = jnp.zeros((8, 8, 128), f32)
        for e in range(EPOCHS):
            across = across_of[v * EPOCHS + e]
            first = pl.multiple_of(starts[v * EPOCHS + e] + 64 * half, 16)
            window = packed[pl.ds(first, 64), :]
            moved = pltpu.roll(window, (-across) & 127, 1).astype(f32).reshape(8, 8, 128)
            source = lane + across
            keep = ((source >= 0) & (source < 128))[None]
            whole = whole + moved
            inside = inside + jnp.where(keep, moved, 0.0)
        outside = whole - inside
        total = inside + jnp.where(from_next, pltpu.roll(outside, 7, 1), 0.0)
        return total + jnp.where(from_last, pltpu.roll(outside, 1, 1), 0.0)

    most = count[0] - 1

    def step(turn, best):
        first, second = 2 * turn, jnp.minimum(2 * turn + 1, most)
        tops = jnp.maximum(best[0], jnp.maximum(stack(first, 0), stack(second, 0)))
        lows = jnp.maximum(best[1], jnp.maximum(stack(first, 1), stack(second, 1)))
        return tops, lows

    least = jnp.full((8, 8, 128), -1e30, f32)
    best = lax.fori_loop(0, (count[0] + 1) // 2, step, (least, least))
    norm = jnp.sqrt(weight_sum)[None]
    for half in range(2):
        table[0, half * 64:half * 64 + 64, :] = (best[half] / norm).reshape(64, 128)
    for q in range(8):
        out[:, q * 128:(q + 1) * 128] = table[0, pl.ds(q, BAND, stride=8), :]


def vmem(count):
    return [pl.BlockSpec(memory_space=pltpu.VMEM)] * count


def smem(count):
    return [pl.BlockSpec(memory_space=pltpu.SMEM)] * count


def shape(*dims, dtype=f32):
    return jax.ShapeDtypeStruct(dims, dtype)


def held(x):
    return pltpu.with_memory_space_constraint(x, pltpu.VMEM)


def to_neighbours(downward, upward):
    tiles = lax.axis_size("sky")
    above = lax.ppermute(downward, "sky", [(i, i + 1) for i in range(tiles - 1)])
    below = lax.ppermute(upward, "sky", [(i + 1, i) for i in range(tiles - 1)])
    return held(above), held(below)


def on_device(visits, template, basis_taps, coeffs, psf_taps, inv_var, shifts, vel_count):
    visits, inv_var, psf = visits[0], inv_var[0], psf_taps[0]
    copies = pl.pallas_call(
        repeat_kernel,
        out_shape=shape(EPOCHS, BAND, W),
        in_specs=[pl.BlockSpec(memory_space=pl.ANY)],
        out_specs=pl.BlockSpec(memory_space=pl.ANY),
        scratch_shapes=[pltpu.SemaphoreType.DMA((EPOCHS,))],
        compiler_params=pltpu.CompilerParams(vmem_limit_bytes=1 << 20),
        name="repeat",
    )(pltpu.with_memory_space_constraint(template, pltpu.HBM))
    bands = lax.all_to_all(copies, "epoch", 0, 0, tiled=True)
    own = jnp.pad(coeffs[0, 0].T, ((0, 5), (0, 128 - NB)))
    wide = jnp.pad(own, ((0, 0), (0, W - 128)))
    above, below = to_neighbours(
        jnp.concatenate([visits[H - VEDGE:], inv_var[H - SMAX:], wide], axis=0),
        jnp.concatenate([visits[:VEDGE], inv_var[:SMAX], wide], axis=0),
    )
    col_taps = jnp.pad(basis_taps[1].T, ((0, 24 - TAPS), (0, 128 - NB)))
    row_taps = jnp.pad(basis_taps[0], ((0, 128 - NB), (0, 128 - TAPS)))
    lhs, weight, inner_rows, outer_rows, col_filter = pl.pallas_call(
        prepare_kernel,
        out_shape=(
            pltpu.VMEM((2, 4 * MID, TAPS * MWIN), bf16),
            shape(8, 128),
            pltpu.VMEM((2 * IROWS, 2 * MID), bf16),
            pltpu.VMEM((2 * OROWS, EWIN), bf16),
            pltpu.VMEM((2, CWIN, NBLK), bf16),
        ),
        in_specs=smem(1) + vmem(4),
        out_specs=tuple(vmem(5)),
        scratch_shapes=[
            pltpu.VMEM((3, 192, 128), f32),
            pltpu.VMEM((2, 2 * MID, TAPS * MWIN), f32),
            pltpu.VMEM((IROWS, 2 * MID), f32),
        ],
        compiler_params=pltpu.CompilerParams(vmem_limit_bytes=8 << 20),
        name="prepare",
    )(psf, held(inv_var), held(own), held(col_taps), held(row_taps))
    bands, weight = lax.optimization_barrier((bands, weight))
    t_above, t_below = to_neighbours(bands[6:].reshape(TEDGE, W), bands[:2].reshape(TEDGE, W))
    filtered, diff_edges, hi_edges, lo_edges = pl.pallas_call(
        inner_kernel,
        out_shape=(
            pltpu.VMEM((IROWS, W), bf16),
            pltpu.VMEM((2 * BAND, W), f32),
            pltpu.VMEM((TAPS, 2 * BAND, W), bf16),
            pltpu.VMEM((TAPS, 2 * BAND, W), bf16),
        ),
        in_specs=vmem(6),
        out_specs=tuple(vmem(4)),
        scratch_shapes=[
            pltpu.VMEM((TAPS, H, W), bf16),
            pltpu.VMEM((TAPS, H, W), bf16),
            pltpu.VMEM((2 * MID, W), f32),
            pltpu.VMEM((2 * IROWS, W + 256), bf16),
        ],
        compiler_params=pltpu.CompilerParams(vmem_limit_bytes=24 << 20),
        name="inner",
    )(held(bands), lhs, held(visits), held(inv_var), inner_rows, col_filter)
    windows = pl.pallas_call(
        outer_kernel,
        out_shape=shape(EPOCHS, OUTR, W, dtype=bf16),
        in_specs=vmem(16),
        out_specs=pl.BlockSpec(memory_space=pl.ANY),
        scratch_shapes=[
            pltpu.VMEM((9, 192, 128), f32),
            pltpu.VMEM((2, 2 * EDGE, TAPS * EWIN), f32),
            pltpu.VMEM((2, 4 * EDGE, TAPS * EWIN), bf16),
            pltpu.VMEM((TAPS, 2 * EWIN, W), bf16),
            pltpu.VMEM((TAPS, 2 * EWIN, W), bf16),
            pltpu.VMEM((2, EWIN, W), f32),
            pltpu.VMEM((4 * OROWS, W + 256), bf16),
            pltpu.VMEM((4, BAND, W), bf16),
            pltpu.VMEM((8, W), bf16),
            pltpu.SemaphoreType.DMA((4 * EPOCHS,)),
        ],
        compiler_params=pltpu.CompilerParams(vmem_limit_bytes=24 << 20),
        name="outer",
    )(held(visits), held(inv_var), above, below, t_above, t_below, filtered, diff_edges, hi_edges, lo_edges,
      held(own), held(col_taps), held(row_taps), held(weight), outer_rows, col_filter)
    down = shifts[0, :, :, 0] + SMAX
    starts = jnp.arange(EPOCHS, dtype=jnp.int32) * 768 + (down & 1) * 384 + (down - (down & 1)) * 8
    moved = lax.all_to_all(windows, "epoch", 0, 0, tiled=True)
    return pl.pallas_call(
        search_kernel,
        out_shape=shape(BAND, W),
        in_specs=smem(3) + vmem(1),
        out_specs=vmem(1)[0],
        scratch_shapes=[pltpu.VMEM((EPOCHS, 384, 128), f32), pltpu.VMEM((2 * EPOCHS * 384, 128), bf16)],
        compiler_params=pltpu.CompilerParams(vmem_limit_bytes=12 << 20),
        name="search",
    )(vel_count, starts.reshape(-1), shifts[0, :, :, 1].reshape(-1), held(moved))


def solution(mesh):
    in_specs = (
        P("epoch", "sky", None),
        P(("sky", "epoch"), None),
        P(),
        P("epoch", "sky", None, None),
        P("epoch", None),
        P("epoch", "sky", None),
        P("sky", None, None, None),
        P("sky"),
    )
    out_specs = P(("sky", "epoch"), None)
    return jax.shard_map(
        on_device, mesh=mesh, in_specs=in_specs, out_specs=out_specs, check_vma=False
    )
```
